256 devices in a mesh: de: 128 (over x, z, y), ha: 2 (over core).
Axes of the slice: x: 4, y: 4, z: 8, core: 2. Of those that a mesh axis runs over, the one named last changes fastest.
Arguments:
- tokens: bfloat16 [16384, 2048], P('de'), may hold values from -6 to 6
- out_grad: bfloat16 [16384, 2048], P('de'), may hold values from -6 to 6
- router_logits: float32 [16384, 128], P('de'), may hold values from -2.5 to 302
- routes: int32 [16384, 8], P('de'), may hold values from 0 to 127, all different within a row; in each aligned block of 128 rows (0 to 127, 128 to 255, ...) at most 10 rows name the same one
- gate_weight: bfloat16 [128, 2048, 768], P('de', None, 'ha'), may hold values from -0.125 to 0.125
- up_weight: bfloat16 [128, 2048, 768], P('de', None, 'ha'), may hold values from -0.125 to 0.125
- down_weight: bfloat16 [128, 768, 2048], P('de', 'ha'), may hold values from -0.21875 to 0.21875
Outputs:
- input_grad: bfloat16 [16384, 2048], P('de')
- logit_grad: float32 [16384, 128], P('de')
- gate_weight_grad: bfloat16 [128, 2048, 768], P('de', None, 'ha')
- up_weight_grad: bfloat16 [128, 2048, 768], P('de', None, 'ha')
- down_weight_grad: bfloat16 [128, 768, 2048], P('de', 'ha')
The draws below stay inside these ranges and needn't reach their ends.
Inputs may be any that keep to these rules, and one draw needn't show every extreme that they name: `routes`: each row names 8 different experts. Among the rows of one device at most 10 name any one expert, and in every draw the rows of some device name some expert exactly 10 times.
All inputs are finite; a program needn't handle non-finite values.
Results may differ from the reference program's by a relative error of at most 0.0071.
Values may be sent and summed in bfloat16 or wider, within the bound.
A program may use at most 128 MiB of HBM per device.

```python
import math
import jax
import jax.numpy as jnp
import numpy as np
from jax import lax

D = 2048
FF = 768
TOP = 8
WIN = 2
TOK_DEV = 128
EXPERTS = 128
TOKENS = 16384
CAP = 10
N_DE = 128
N_HA = 2


def draw_router_logits(key, part):
    base_key = jax.random.fold_in(jax.random.fold_in(key, 7), 0)
    logits = 0.8 * jax.random.truncated_normal(base_key, -3.0, 3.0, (TOKENS, EXPERTS), jnp.float32)
    return logits


def shard_levels(key, dims, cuts, least, high):
    def one(dim, parts):
        steps = jax.random.uniform(jax.random.fold_in(jax.random.fold_in(key, 6), dim), (parts,), jnp.float32, least / len(cuts), high / len(cuts))
        return jnp.repeat(jnp.exp(steps), dims[dim] // parts).reshape((-1,) + (1,) * (len(dims) - dim - 1))

    factor_of = one(*cuts[0])
    for cut in cuts[1:]:
        factor_of = factor_of * one(*cut)
    return factor_of


def deal_out(own_key, own, number, rows, number_of, top, bound, skew):
    ranking = jax.random.permutation(own_key, number_of)
    crowded, common = shares(number_of, rows * top, bound, skew, True), shares(number_of, rows * top, bound, skew, False)
    places = jnp.arange(number_of)

    def named(lengths, rotation):
        used = int((lengths > 0).sum())
        fixed = max(1, used // 4)
        moved = fixed + (places - fixed + rotation * (used - fixed)) % max(1, number_of - fixed)
        return jnp.zeros((number_of,), jnp.int32).at[ranking[jnp.where(places < fixed, places, moved)]].set(jnp.asarray(lengths, jnp.int32))

    lengths = jnp.where(number % 4 == 0, named(crowded, number // 4), named(common, number - number // 4 - 1))
    mixed = jax.random.permutation(jax.random.fold_in(own, 3), number_of)
    source_of, receiver = mixed[0:number_of // 2 * 2:2], mixed[1:number_of // 2 * 2:2]
    margin = jnp.minimum(lengths[source_of] - 1, bound - lengths[receiver]) // 2
    margin = jnp.where((source_of == ranking[0]) | (receiver == ranking[0]) | (lengths[receiver] == 0), 0, jnp.maximum(margin, 0))
    moved = jax.random.randint(jax.random.fold_in(own, 4), (number_of // 2,), 0, 1 << 20) % (margin + 1)
    lengths = lengths.at[source_of].add(-moved).at[receiver].add(moved)
    items = jnp.searchsorted(jnp.cumsum(lengths), jnp.arange(rows * top), side="right").astype(jnp.int32)
    listing = items.reshape(top, rows).T
    listing = listing[jax.random.permutation(jax.random.fold_in(own, 1), rows)]
    rotation = jax.random.randint(jax.random.fold_in(own, 2), (rows, 1), 0, top)
    return jnp.take_along_axis(listing, (jnp.arange(top)[None, :] + rotation) % top, axis=1)


def shares(number_of, total, reach, slope, full):
    loads = [(1 << 20) // math.isqrt(standing ** slope) + 1 for standing in range(1, number_of + 1)]
    largest = reach if full else min(reach, max(-(-total // number_of), total * loads[0] // sum(loads)))
    least = 1 if total - largest >= number_of - 1 else 0
    given, rest = [largest] + [least] * (number_of - 1), total - largest - least * (number_of - 1)
    while rest > 0:
        candidates = [i for i in range(1, number_of) if given[i] < largest] or [i for i in range(1, number_of) if given[i] < reach]
        whole, left = sum([loads[i] for i in candidates]), rest
        for i in candidates:
            extra = min(reach - given[i], max(1, left * loads[i] // whole), rest)
            given[i] = given[i] + extra
            rest = rest - extra
    return np.array(given)


def gaussian(key, shape, deviation, reach, cuts=(), kind=jnp.bfloat16):
    drawn = deviation * jax.random.normal(key, shape, jnp.float32)
    if cuts:
        drawn = drawn * shard_levels(key, shape, cuts, -0.22, 0.18)
    return jnp.clip(drawn, -reach, reach).astype(kind)


def setup_inputs(seed: int = 0) -> dict:
    splits = jax.random.split(jax.random.key(seed), 8)
    tokens = gaussian(splits[0], (TOKENS, D), 1.0, 6.0, ((0, 128),))
    out_grad = gaussian(splits[1], (TOKENS, D), 1.0, 6.0, ((0, 128),))
    router_logits = draw_router_logits(jax.random.fold_in(splits[7], 71), 0)
    routes_keys = jax.random.split(jax.random.fold_in(splits[3], 1), TOKENS // TOK_DEV)
    routes_turns = jax.random.permutation(jax.random.fold_in(splits[3], 3), TOKENS // TOK_DEV)
    routes = jax.vmap(lambda own, number: deal_out(jax.random.fold_in(splits[3], 2), own, number, TOK_DEV, EXPERTS, TOP, CAP, 2))(routes_keys, routes_turns).reshape((TOKENS, TOP))
    gate_weight = gaussian(splits[4], (EXPERTS, D, FF), D ** -0.5, 0.125, ((0, 128), (2, 2)))
    up_weight = gaussian(splits[5], (EXPERTS, D, FF), D ** -0.5, 0.125, ((0, 128), (2, 2)))
    down_weight = gaussian(splits[6], (EXPERTS, FF, D), FF ** -0.5, 0.21875, ((0, 128), (1, 2)))
    return dict(tokens=tokens, out_grad=out_grad, router_logits=router_logits, routes=routes, gate_weight=gate_weight, up_weight=up_weight, down_weight=down_weight)


def expert_rows(rows_in, grads_in, weight_in, w_gate, w_up, w_down):
    half_units = FF // N_HA
    dot_sum = jnp.zeros((rows_in.shape[0],), jnp.float32)
    input_sum = jnp.zeros(rows_in.shape, jnp.float32)
    gate_parts = []
    up_parts = []
    down_parts = []
    for core_index in range(N_HA):
        start_col = core_index * half_units
        gate_cols = w_gate[:, start_col:start_col + half_units]
        up_cols = w_up[:, start_col:start_col + half_units]
        down_rows = w_down[start_col:start_col + half_units, :]
        pre_gate = jnp.dot(rows_in, gate_cols, preferred_element_type=jnp.float32)
        pre_up = jnp.dot(rows_in, up_cols, preferred_element_type=jnp.float32)
        sig_gate = jax.nn.sigmoid(pre_gate)
        silu_gate = pre_gate * sig_gate
        hidden_act = silu_gate * pre_up
        back_grad = lax.dot_general(grads_in, down_rows, (((1,), (1,)), ((), ())), preferred_element_type=jnp.float32)
        dot_sum = dot_sum + jnp.sum(hidden_act * back_grad, axis=-1)
        scaled_back = weight_in[:, None] * back_grad
        scaled_act = (weight_in[:, None] * hidden_act).astype(jnp.bfloat16)
        grad_gate = (scaled_back * pre_up * sig_gate * (1.0 + pre_gate * (1.0 - sig_gate))).astype(jnp.bfloat16)
        grad_up = (scaled_back * silu_gate).astype(jnp.bfloat16)
        gate_parts.append(lax.dot_general(rows_in, grad_gate, (((0,), (0,)), ((), ())), preferred_element_type=jnp.float32))
        up_parts.append(lax.dot_general(rows_in, grad_up, (((0,), (0,)), ((), ())), preferred_element_type=jnp.float32))
        down_parts.append(lax.dot_general(scaled_act, grads_in, (((0,), (0,)), ((), ())), preferred_element_type=jnp.float32))
        partial_input = lax.dot_general(grad_gate, gate_cols, (((1,), (1,)), ((), ())), preferred_element_type=jnp.float32)
        partial_input = partial_input + lax.dot_general(grad_up, up_cols, (((1,), (1,)), ((), ())), preferred_element_type=jnp.float32)
        rounded_part = lax.optimization_barrier(partial_input.astype(jnp.bfloat16))
        input_sum = input_sum + rounded_part.astype(jnp.float32)
    gate_grad = jnp.concatenate(gate_parts, axis=1)
    up_grad = jnp.concatenate(up_parts, axis=1)
    down_grad = jnp.concatenate(down_parts, axis=0)
    return input_sum, dot_sum, gate_grad, up_grad, down_grad


def reference(tokens, out_grad, router_logits, routes, gate_weight, up_weight, down_weight):
    router_probs = jax.nn.softmax(router_logits, axis=-1)
    route_total = TOKENS * TOP
    flat_expert = routes.reshape(-1)
    route_weight = jnp.take_along_axis(router_probs, routes, axis=1).astype(jnp.bfloat16).reshape(-1)
    sorted_routes = jnp.argsort(flat_expert, stable=True).astype(jnp.int32)
    expert_ids = jnp.arange(EXPERTS, dtype=jnp.int32)
    counts = jnp.sum((flat_expert[None, :] == expert_ids[:, None]).astype(jnp.int32), axis=1).astype(jnp.int32)
    starts = (jnp.cumsum(counts) - counts).astype(jnp.int32)
    row_limit = N_DE * CAP
    padded_routes = jnp.concatenate([sorted_routes, jnp.full((row_limit,), route_total, jnp.int32)])
    padded_tokens = jnp.concatenate([tokens, jnp.zeros((1, D), tokens.dtype)])
    padded_grads = jnp.concatenate([out_grad, jnp.zeros((1, D), out_grad.dtype)])
    padded_weight = jnp.concatenate([route_weight, jnp.zeros((1,), route_weight.dtype)])

    def one_expert(loop_state, inputs):
        input_acc, dot_table = loop_state
        expert, w_gate, w_up, w_down = inputs
        picked = lax.dynamic_slice(padded_routes, (starts[expert],), (row_limit,))
        live_row = jnp.arange(row_limit, dtype=jnp.int32) < counts[expert]
        picked = jnp.where(live_row, picked, route_total).astype(jnp.int32)
        token_row = (picked // TOP).astype(jnp.int32)
        rows_in = padded_tokens[token_row]
        grads_in = padded_grads[token_row]
        weight_in = padded_weight[picked].astype(jnp.float32)
        input_sum, dot_sum, gate_grad, up_grad, down_grad = expert_rows(rows_in, grads_in, weight_in, w_gate, w_up, w_down)
        route_input = lax.optimization_barrier(input_sum.astype(jnp.bfloat16)).astype(jnp.float32)
        route_dot = lax.optimization_barrier(dot_sum.astype(jnp.bfloat16)).astype(jnp.float32)
        input_acc = input_acc.at[token_row].add(jnp.where(live_row[:, None], route_input, 0.0), mode="drop")
        dot_table = dot_table.at[token_row, expert].add(jnp.where(live_row, route_dot, 0.0), mode="drop")
        return (input_acc, dot_table), (gate_grad.astype(jnp.bfloat16), up_grad.astype(jnp.bfloat16), down_grad.astype(jnp.bfloat16))

    start_state = (jnp.zeros((TOKENS, D), jnp.float32), jnp.zeros((TOKENS, EXPERTS), jnp.float32))
    final_state, stacked = lax.scan(one_expert, start_state, (expert_ids, gate_weight, up_weight, down_weight))
    input_acc, dot_table = final_state
    gate_grads, up_grads, down_grads = stacked
    stride = EXPERTS // WIN
    for window in range(WIN):
        expert = window * stride
        pre_gate = jnp.dot(tokens, gate_weight[expert], preferred_element_type=jnp.float32)
        pre_up = jnp.dot(tokens, up_weight[expert], preferred_element_type=jnp.float32)
        hidden_act = pre_gate * jax.nn.sigmoid(pre_gate) * pre_up
        back_grad = lax.dot_general(out_grad, down_weight[expert], (((1,), (1,)), ((), ())), preferred_element_type=jnp.float32)
        dense_dot = jnp.sum(hidden_act * back_grad, axis=-1)
        dot_table = dot_table.at[:, expert].set(dense_dot)
    logit_grad = router_probs * (dot_table - jnp.sum(router_probs * dot_table, axis=-1, keepdims=True))
    return (input_acc.astype(jnp.bfloat16), logit_grad, gate_grads, up_grads, down_grads)
```

```python
import jax
import jax.numpy as jnp
from jax import lax
from jax.sharding import PartitionSpec as P

WIN = 2
DOT_COLS = 128


def spread(value, axis, source):
    kept = jnp.where(lax.axis_index(axis) == source, value, 0).astype(value.dtype)
    return lax.psum(kept, axis)


def owner_pass(rows_in, grads_in, weight_in, w_gate, w_up, w_down):
    pre_gate = jnp.dot(rows_in, w_gate, preferred_element_type=jnp.float32)
    pre_up = jnp.dot(rows_in, w_up, preferred_element_type=jnp.float32)
    sig_gate = jax.nn.sigmoid(pre_gate)
    silu_gate = pre_gate * sig_gate
    hidden_act = silu_gate * pre_up
    back_grad = lax.dot_general(
        grads_in, w_down, (((1,), (1,)), ((), ())), preferred_element_type=jnp.float32
    )
    row_dots = jnp.sum(hidden_act * back_grad, axis=-1)
    scaled_back = weight_in[:, None] * back_grad
    scaled_act = (weight_in[:, None] * hidden_act).astype(jnp.bfloat16)
    grad_gate = (scaled_back * pre_up * sig_gate * (1.0 + pre_gate * (1.0 - sig_gate))).astype(
        jnp.bfloat16
    )
    grad_up = (scaled_back * silu_gate).astype(jnp.bfloat16)
    sum_gate = lax.dot_general(
        rows_in, grad_gate, (((0,), (0,)), ((), ())), preferred_element_type=jnp.float32
    )
    sum_up = lax.dot_general(
        rows_in, grad_up, (((0,), (0,)), ((), ())), preferred_element_type=jnp.float32
    )
    sum_down = lax.dot_general(
        scaled_act, grads_in, (((0,), (0,)), ((), ())), preferred_element_type=jnp.float32
    )
    partial_input = lax.dot_general(
        grad_gate, w_gate, (((1,), (1,)), ((), ())), preferred_element_type=jnp.float32
    )
    partial_input = partial_input + lax.dot_general(
        grad_up, w_up, (((1,), (1,)), ((), ())), preferred_element_type=jnp.float32
    )
    return (partial_input, row_dots, sum_gate, sum_up, sum_down)


def per_device(tokens, out_grad, router_logits, routes, gate_weight, up_weight, down_weight):
    n_dev = lax.axis_size("de")
    n_ha = lax.axis_size("ha")
    core = lax.axis_index("ha")
    tok_rows, model_width = tokens.shape
    route_count = routes.shape[1]
    experts = n_dev * gate_weight.shape[0]
    slot_count = max(2, 5 * tok_rows * route_count // (4 * experts))
    half = -(-slot_count // n_ha)
    slot_count = half * n_ha
    feat = model_width // n_ha
    w_gate = gate_weight[0]
    w_up = up_weight[0]
    w_down = down_weight[0]
    router_probs = jax.nn.softmax(router_logits, axis=-1)
    stride = n_dev // WIN
    dense_cols = []
    for window in range(WIN):
        sent_gate, sent_up, sent_down = (
            spread(w_gate, "de", window * stride),
            spread(w_up, "de", window * stride),
            spread(w_down, "de", window * stride),
        )
        pre_gate = jnp.dot(tokens, sent_gate, preferred_element_type=jnp.float32)
        pre_up = jnp.dot(tokens, sent_up, preferred_element_type=jnp.float32)
        hidden_act = pre_gate * jax.nn.sigmoid(pre_gate) * pre_up
        back_grad = lax.dot_general(
            out_grad, sent_down, (((1,), (1,)), ((), ())), preferred_element_type=jnp.float32
        )
        dense_cols.append(jnp.sum(hidden_act * back_grad, axis=-1))
    dense_dots = lax.psum(jnp.stack(dense_cols, axis=1), "ha")
    route_total = tok_rows * route_count
    total_slots = experts * slot_count
    flat_expert = routes.reshape(-1)
    expert_ids = jnp.arange(experts, dtype=jnp.int32)
    onehot = (flat_expert[:, None] == expert_ids[None, :]).astype(jnp.int32)
    ranking = jnp.sum(jnp.cumsum(onehot, axis=0) * onehot, axis=1) - 1
    slot_of_route = flat_expert * slot_count + ranking
    route_of_slot = (
        jnp.full((total_slots,), route_total, jnp.int32)
        .at[slot_of_route]
        .set(jnp.arange(route_total, dtype=jnp.int32))
    )
    my_routes = lax.dynamic_index_in_dim(
        route_of_slot.reshape(experts, n_ha, half), core, axis=1, keepdims=False
    )
    my_tokens = my_routes // route_count
    route_weight = (
        jnp.take_along_axis(router_probs, routes, axis=1).astype(jnp.bfloat16).reshape(-1)
    )
    padded_tokens = jnp.concatenate([tokens, jnp.zeros((1, model_width), tokens.dtype)])
    padded_grads = jnp.concatenate([out_grad, jnp.zeros((1, model_width), out_grad.dtype)])
    padded_weight = jnp.concatenate([route_weight, jnp.zeros((1,), route_weight.dtype)])
    send_xg = jnp.concatenate([padded_tokens[my_tokens], padded_grads[my_tokens]], axis=1)
    send_weight = padded_weight[my_routes]
    recv_xg = lax.all_to_all(send_xg, "de", split_axis=0, concat_axis=0, tiled=True)
    recv_weight = lax.all_to_all(send_weight, "de", split_axis=0, concat_axis=0, tiled=True)
    all_xg = lax.all_gather(recv_xg, "ha", axis=0, tiled=False)
    all_weight = lax.all_gather(recv_weight, "ha", axis=0, tiled=False)
    rows_in = all_xg[:, :, :half].reshape(-1, model_width)
    grads_in = all_xg[:, :, half:].reshape(-1, model_width)
    weight_in = all_weight.reshape(-1).astype(jnp.float32)
    input_slot, dot_slot, sum_gate, sum_up, sum_down = owner_pass(
        rows_in, grads_in, weight_in, w_gate, w_up, w_down
    )
    dot_slot = lax.psum(dot_slot, "ha")
    input_half = lax.psum_scatter(
        input_slot.reshape(n_ha, n_dev, half, model_width).astype(jnp.bfloat16),
        "ha",
        scatter_dimension=3,
        tiled=True,
    )
    dot_back = jnp.broadcast_to(
        dot_slot.astype(jnp.bfloat16).reshape(n_ha, n_dev, half, 1), (n_ha, n_dev, half, DOT_COLS)
    )
    ret = jnp.concatenate([input_half, dot_back], axis=3)
    ret = jnp.transpose(ret, (1, 0, 2, 3)).reshape(n_dev, slot_count, feat + DOT_COLS)
    back = lax.all_to_all(ret, "de", split_axis=0, concat_axis=0, tiled=True)
    back = back.reshape(total_slots, feat + DOT_COLS)[slot_of_route]
    route_input = back[:, :feat].astype(jnp.float32)
    input_part = jnp.sum(route_input.reshape(tok_rows, route_count, feat), axis=1).astype(
        jnp.bfloat16
    )
    input_grad = lax.all_gather(input_part, "ha", axis=1, tiled=True)
    route_dots = back[:, feat].astype(jnp.float32).reshape(tok_rows, route_count)
    dot_table = jnp.sum(
        jnp.where(routes[:, :, None] == expert_ids[None, None, :], route_dots[:, :, None], 0.0),
        axis=1,
    )
    for window in range(WIN):
        dot_table = jnp.where(
            expert_ids[None, :] == window * stride, dense_dots[:, window : window + 1], dot_table
        )
    logit_grad = router_probs * (
        dot_table - jnp.sum(router_probs * dot_table, axis=-1, keepdims=True)
    )
    return (
        input_grad,
        logit_grad,
        sum_gate.astype(jnp.bfloat16)[None],
        sum_up.astype(jnp.bfloat16)[None],
        sum_down.astype(jnp.bfloat16)[None],
    )


def solution(mesh):
    return jax.shard_map(
        per_device,
        mesh=mesh,
        in_specs=(
            P("de", None),
            P("de", None),
            P("de", None),
            P("de", None),
            P("de", None, "ha"),
            P("de", None, "ha"),
            P("de", "ha", None),
        ),
        out_specs=(
            P("de", None),
            P("de", None),
            P("de", None, "ha"),
            P("de", None, "ha"),
            P("de", "ha", None),
        ),
        check_vma=False,
    )
```

```python
import jax
import jax.numpy as jnp
from jax import lax
from jax.sharding import PartitionSpec as P


WIN = 2
DOT_COLS = 128


def spread(value, axis, source):
    kept = jnp.where(lax.axis_index(axis) == source, value, 0).astype(value.dtype)
    return lax.psum(kept, axis)


def owner_pass(rows_in, grads_in, weight_in, w_gate, w_up, w_down):
    pre_gate = jnp.dot(rows_in, w_gate, preferred_element_type=jnp.float32)
    pre_up = jnp.dot(rows_in, w_up, preferred_element_type=jnp.float32)
    sig_gate = jax.nn.sigmoid(pre_gate)
    silu_gate = pre_gate * sig_gate
    hidden_act = silu_gate * pre_up
    back_grad = lax.dot_general(
        grads_in, w_down, (((1,), (1,)), ((), ())), preferred_element_type=jnp.float32
    )
    row_dots = jnp.sum(hidden_act * back_grad, axis=-1)
    scaled_back = weight_in[:, None] * back_grad
    scaled_act = (weight_in[:, None] * hidden_act).astype(jnp.bfloat16)
    grad_gate = (scaled_back * pre_up * sig_gate * (1.0 + pre_gate * (1.0 - sig_gate))).astype(
        jnp.bfloat16
    )
    grad_up = (scaled_back * silu_gate).astype(jnp.bfloat16)
    sum_gate = lax.dot_general(
        rows_in, grad_gate, (((0,), (0,)), ((), ())), preferred_element_type=jnp.float32
    )
    sum_up = lax.dot_general(
        rows_in, grad_up, (((0,), (0,)), ((), ())), preferred_element_type=jnp.float32
    )
    sum_down = lax.dot_general(
        scaled_act, grads_in, (((0,), (0,)), ((), ())), preferred_element_type=jnp.float32
    )
    partial_input = lax.dot_general(
        grad_gate, w_gate, (((1,), (1,)), ((), ())), preferred_element_type=jnp.float32
    )
    partial_input = partial_input + lax.dot_general(
        grad_up, w_up, (((1,), (1,)), ((), ())), preferred_element_type=jnp.float32
    )
    return (partial_input, row_dots, sum_gate, sum_up, sum_down)


def layer(tokens, out_grad, router_logits, routes, gate_weight, up_weight, down_weight):
    n_dev = lax.axis_size("de")
    n_ha = lax.axis_size("ha")
    core = lax.axis_index("ha")
    tok_rows, model_width = tokens.shape
    route_count = routes.shape[1]
    experts = n_dev * gate_weight.shape[0]
    slot_count = max(2, 5 * tok_rows * route_count // (4 * experts))
    half = -(-slot_count // n_ha)
    slot_count = half * n_ha
    feat = model_width // n_ha
    w_gate = gate_weight[0]
    w_up = up_weight[0]
    w_down = down_weight[0]
    router_probs = jax.nn.softmax(router_logits, axis=-1)
    stride = n_dev // WIN
    dense_cols = []
    for window in range(WIN):
        sent_gate, sent_up, sent_down = (
            spread(w_gate, "de", window * stride),
            spread(w_up, "de", window * stride),
            spread(w_down, "de", window * stride),
        )
        pre_gate = jnp.dot(tokens, sent_gate, preferred_element_type=jnp.float32)
        pre_up = jnp.dot(tokens, sent_up, preferred_element_type=jnp.float32)
        hidden_act = pre_gate * jax.nn.sigmoid(pre_gate) * pre_up
        back_grad = lax.dot_general(
            out_grad, sent_down, (((1,), (1,)), ((), ())), preferred_element_type=jnp.float32
        )
        dense_cols.append(jnp.sum(hidden_act * back_grad, axis=-1))
    dense_dots = lax.psum(jnp.stack(dense_cols, axis=1), "ha")
    route_total = tok_rows * route_count
    total_slots = experts * slot_count
    flat_expert = routes.reshape(-1)
    expert_ids = jnp.arange(experts, dtype=jnp.int32)
    onehot = (flat_expert[:, None] == expert_ids[None, :]).astype(jnp.int32)
    ranking = jnp.sum(jnp.cumsum(onehot, axis=0) * onehot, axis=1) - 1
    slot_of_route = flat_expert * slot_count + ranking
    route_of_slot = (
        jnp.full((total_slots,), route_total, jnp.int32)
        .at[slot_of_route]
        .set(jnp.arange(route_total, dtype=jnp.int32))
    )
    my_routes = lax.dynamic_index_in_dim(
        route_of_slot.reshape(experts, n_ha, half), core, axis=1, keepdims=False
    )
    my_tokens = my_routes // route_count
    route_weight = (
        jnp.take_along_axis(router_probs, routes, axis=1).astype(jnp.bfloat16).reshape(-1)
    )
    padded_tokens = jnp.concatenate([tokens, jnp.zeros((1, model_width), tokens.dtype)])
    padded_grads = jnp.concatenate([out_grad, jnp.zeros((1, model_width), out_grad.dtype)])
    padded_weight = jnp.concatenate([route_weight, jnp.zeros((1,), route_weight.dtype)])
    send_x = padded_tokens[my_tokens]
    send_g = padded_grads[my_tokens]
    send_weight = padded_weight[my_routes]
    recv_x = lax.all_to_all(send_x, "de", split_axis=0, concat_axis=0, tiled=True)
    recv_g = lax.all_to_all(send_g, "de", split_axis=0, concat_axis=0, tiled=True)
    recv_weight = lax.all_to_all(send_weight, "de", split_axis=0, concat_axis=0, tiled=True)
    rows_in = lax.all_gather(recv_x, "ha", axis=0, tiled=True).reshape(-1, model_width)
    grads_in = lax.all_gather(recv_g, "ha", axis=0, tiled=True).reshape(-1, model_width)
    all_weight = lax.all_gather(recv_weight, "ha", axis=0, tiled=True)
    weight_in = all_weight.reshape(-1).astype(jnp.float32)
    input_slot, dot_slot, sum_gate, sum_up, sum_down = owner_pass(
        rows_in, grads_in, weight_in, w_gate, w_up, w_down
    )
    dot_slot = lax.psum(dot_slot, "ha")
    input_half = lax.psum_scatter(
        input_slot.reshape(n_ha, n_dev, half, model_width).astype(jnp.bfloat16),
        "ha",
        scatter_dimension=3,
        tiled=True,
    )
    dot_back = jnp.broadcast_to(
        dot_slot.astype(jnp.bfloat16).reshape(n_ha, n_dev, half, 1), (n_ha, n_dev, half, DOT_COLS)
    )
    ret = jnp.concatenate([input_half, dot_back], axis=3)
    ret = jnp.transpose(ret, (1, 0, 2, 3)).reshape(n_dev, slot_count, feat + DOT_COLS)
    back = lax.all_to_all(ret, "de", split_axis=0, concat_axis=0, tiled=True)
    back = back.reshape(total_slots, feat + DOT_COLS)[slot_of_route]
    route_input = back[:, :feat].astype(jnp.float32)
    input_part = jnp.sum(route_input.reshape(tok_rows, route_count, feat), axis=1).astype(
        jnp.bfloat16
    )
    input_grad = lax.all_gather(input_part, "ha", axis=1, tiled=True)
    route_dots = back[:, feat].astype(jnp.float32).reshape(tok_rows, route_count)
    dot_table = jnp.sum(
        jnp.where(routes[:, :, None] == expert_ids[None, None, :], route_dots[:, :, None], 0.0),
        axis=1,
    )
    for window in range(WIN):
        dot_table = jnp.where(
            expert_ids[None, :] == window * stride, dense_dots[:, window : window + 1], dot_table
        )
    logit_grad = router_probs * (
        dot_table - jnp.sum(router_probs * dot_table, axis=-1, keepdims=True)
    )
    return (
        input_grad,
        logit_grad,
        sum_gate.astype(jnp.bfloat16)[None],
        sum_up.astype(jnp.bfloat16)[None],
        sum_down.astype(jnp.bfloat16)[None],
    )


def solution(mesh):
    return jax.shard_map(
        layer,
        mesh=mesh,
        in_specs=(
            P("de", None),
            P("de", None),
            P("de", None),
            P("de", None),
            P("de", None, "ha"),
            P("de", None, "ha"),
            P("de", "ha", None),
        ),
        out_specs=(
            P("de", None),
            P("de", None),
            P("de", None, "ha"),
            P("de", None, "ha"),
            P("de", "ha", None),
        ),
        check_vma=False,
    )
```

```python
import jax
import jax.numpy as jnp
from jax import lax
from jax.sharding import PartitionSpec as P


WIN = 2
DOT_COLS = 128


def spread(value, axis, source):
    kept = jnp.where(lax.axis_index(axis) == source, value, 0).astype(value.dtype)
    return lax.psum(kept, axis)


def share_halves(mine, core, n_ha):
    other = lax.ppermute(mine, "ha", [(i, (i + 1) % n_ha) for i in range(n_ha)])
    full = jnp.zeros((n_ha,) + mine.shape, mine.dtype)
    full = lax.dynamic_update_index_in_dim(full, mine, core, 0)
    return lax.dynamic_update_index_in_dim(full, other, 1 - core, 0)


def owner_pass(rows_in, grads_in, weight_in, w_gate, w_up, w_down):
    pre_gate = jnp.dot(rows_in, w_gate, preferred_element_type=jnp.float32)
    pre_up = jnp.dot(rows_in, w_up, preferred_element_type=jnp.float32)
    sig_gate = jax.nn.sigmoid(pre_gate)
    silu_gate = pre_gate * sig_gate
    hidden_act = silu_gate * pre_up
    back_grad = lax.dot_general(
        grads_in, w_down, (((1,), (1,)), ((), ())), preferred_element_type=jnp.float32
    )
    row_dots = jnp.sum(hidden_act * back_grad, axis=-1)
    scaled_back = weight_in[:, None] * back_grad
    scaled_act = (weight_in[:, None] * hidden_act).astype(jnp.bfloat16)
    grad_gate = (scaled_back * pre_up * sig_gate * (1.0 + pre_gate * (1.0 - sig_gate))).astype(
        jnp.bfloat16
    )
    grad_up = (scaled_back * silu_gate).astype(jnp.bfloat16)
    sum_gate = lax.dot_general(
        rows_in, grad_gate, (((0,), (0,)), ((), ())), preferred_element_type=jnp.float32
    )
    sum_up = lax.dot_general(
        rows_in, grad_up, (((0,), (0,)), ((), ())), preferred_element_type=jnp.float32
    )
    sum_down = lax.dot_general(
        scaled_act, grads_in, (((0,), (0,)), ((), ())), preferred_element_type=jnp.float32
    )
    partial_input = lax.dot_general(
        grad_gate, w_gate, (((1,), (1,)), ((), ())), preferred_element_type=jnp.float32
    )
    partial_input = partial_input + lax.dot_general(
        grad_up, w_up, (((1,), (1,)), ((), ())), preferred_element_type=jnp.float32
    )
    return (partial_input, row_dots, sum_gate, sum_up, sum_down)


def layer(tokens, out_grad, router_logits, routes, gate_weight, up_weight, down_weight):
    n_dev = lax.axis_size("de")
    n_ha = lax.axis_size("ha")
    core = lax.axis_index("ha")
    tok_rows, model_width = tokens.shape
    route_count = routes.shape[1]
    experts = n_dev * gate_weight.shape[0]
    slot_count = max(2, 5 * tok_rows * route_count // (4 * experts))
    half = -(-slot_count // n_ha)
    slot_count = half * n_ha
    feat = model_width // n_ha
    w_gate = gate_weight[0]
    w_up = up_weight[0]
    w_down = down_weight[0]
    router_probs = jax.nn.softmax(router_logits, axis=-1)
    stride = n_dev // WIN
    dense_cols = []
    for window in range(WIN):
        sent_gate, sent_up, sent_down = (
            spread(w_gate, "de", window * stride),
            spread(w_up, "de", window * stride),
            spread(w_down, "de", window * stride),
        )
        pre_gate = jnp.dot(tokens, sent_gate, preferred_element_type=jnp.float32)
        pre_up = jnp.dot(tokens, sent_up, preferred_element_type=jnp.float32)
        hidden_act = pre_gate * jax.nn.sigmoid(pre_gate) * pre_up
        back_grad = lax.dot_general(
            out_grad, sent_down, (((1,), (1,)), ((), ())), preferred_element_type=jnp.float32
        )
        dense_cols.append(jnp.sum(hidden_act * back_grad, axis=-1))
    dense_dots = lax.psum(jnp.stack(dense_cols, axis=1), "ha")
    route_total = tok_rows * route_count
    total_slots = experts * slot_count
    flat_expert = routes.reshape(-1)
    expert_ids = jnp.arange(experts, dtype=jnp.int32)
    onehot = (flat_expert[:, None] == expert_ids[None, :]).astype(jnp.int32)
    ranking = jnp.sum(jnp.cumsum(onehot, axis=0) * onehot, axis=1) - 1
    slot_of_route = flat_expert * slot_count + ranking
    route_of_slot = (
        jnp.full((total_slots,), route_total, jnp.int32)
        .at[slot_of_route]
        .set(jnp.arange(route_total, dtype=jnp.int32))
    )
    my_routes = lax.dynamic_index_in_dim(
        route_of_slot.reshape(experts, n_ha, half), core, axis=1, keepdims=False
    )
    my_tokens = my_routes // route_count
    route_weight = (
        jnp.take_along_axis(router_probs, routes, axis=1).astype(jnp.bfloat16).reshape(-1)
    )
    padded_tokens = jnp.concatenate([tokens, jnp.zeros((1, model_width), tokens.dtype)])
    padded_grads = jnp.concatenate([out_grad, jnp.zeros((1, model_width), out_grad.dtype)])
    padded_weight = jnp.concatenate([route_weight, jnp.zeros((1,), route_weight.dtype)])
    send_x = padded_tokens[my_tokens]
    send_g = padded_grads[my_tokens]
    send_weight = padded_weight[my_routes]
    recv_x = lax.all_to_all(send_x, "de", split_axis=0, concat_axis=0, tiled=True)
    recv_g = lax.all_to_all(send_g, "de", split_axis=0, concat_axis=0, tiled=True)
    recv_weight = lax.all_to_all(send_weight, "de", split_axis=0, concat_axis=0, tiled=True)
    rows_in = share_halves(recv_x, core, n_ha).reshape(-1, model_width)
    grads_in = share_halves(recv_g, core, n_ha).reshape(-1, model_width)
    all_weight = share_halves(recv_weight, core, n_ha)
    weight_in = all_weight.reshape(-1).astype(jnp.float32)
    input_slot, dot_slot, sum_gate, sum_up, sum_down = owner_pass(
        rows_in, grads_in, weight_in, w_gate, w_up, w_down
    )
    dot_slot = lax.psum(dot_slot, "ha")
    input_half = lax.psum_scatter(
        input_slot.reshape(n_ha, n_dev, half, model_width).astype(jnp.bfloat16),
        "ha",
        scatter_dimension=3,
        tiled=True,
    )
    dot_back = jnp.broadcast_to(
        dot_slot.astype(jnp.bfloat16).reshape(n_ha, n_dev, half, 1), (n_ha, n_dev, half, DOT_COLS)
    )
    ret = jnp.concatenate([input_half, dot_back], axis=3)
    ret = jnp.transpose(ret, (1, 0, 2, 3)).reshape(n_dev, slot_count, feat + DOT_COLS)
    back = lax.all_to_all(ret, "de", split_axis=0, concat_axis=0, tiled=True)
    back = back.reshape(total_slots, feat + DOT_COLS)[slot_of_route]
    route_input = back[:, :feat].astype(jnp.float32)
    input_part = jnp.sum(route_input.reshape(tok_rows, route_count, feat), axis=1).astype(
        jnp.bfloat16
    )
    input_grad = lax.all_gather(input_part, "ha", axis=1, tiled=True)
    route_dots = back[:, feat].astype(jnp.float32).reshape(tok_rows, route_count)
    dot_table = jnp.sum(
        jnp.where(routes[:, :, None] == expert_ids[None, None, :], route_dots[:, :, None], 0.0),
        axis=1,
    )
    for window in range(WIN):
        dot_table = jnp.where(
            expert_ids[None, :] == window * stride, dense_dots[:, window : window + 1], dot_table
        )
    logit_grad = router_probs * (
        dot_table - jnp.sum(router_probs * dot_table, axis=-1, keepdims=True)
    )
    return (
        input_grad,
        logit_grad,
        sum_gate.astype(jnp.bfloat16)[None],
        sum_up.astype(jnp.bfloat16)[None],
        sum_down.astype(jnp.bfloat16)[None],
    )


def solution(mesh):
    return jax.shard_map(
        layer,
        mesh=mesh,
        in_specs=(
            P("de", None),
            P("de", None),
            P("de", None),
            P("de", None),
            P("de", None, "ha"),
            P("de", None, "ha"),
            P("de", "ha", None),
        ),
        out_specs=(
            P("de", None),
            P("de", None),
            P("de", None, "ha"),
            P("de", None, "ha"),
            P("de", "ha", None),
        ),
        check_vma=False,
    )
```

```python
import jax
import jax.numpy as jnp
from jax import lax
from jax.sharding import PartitionSpec as P


WIN = 2
DOT_COLS = 128


def spread(value, axis, source):
    kept = jnp.where(lax.axis_index(axis) == source, value, 0).astype(value.dtype)
    return lax.psum(kept, axis)


def share_halves(mine, core, n_ha):
    other = lax.ppermute(mine, "ha", [(i, (i + 1) % n_ha) for i in range(n_ha)])
    full = jnp.zeros((n_ha,) + mine.shape, mine.dtype)
    full = lax.dynamic_update_index_in_dim(full, mine, core, 0)
    return lax.dynamic_update_index_in_dim(full, other, 1 - core, 0)


def owner_pass(rows_in, grads_in, weight_in, w_gate, w_up, w_down):
    pre_gate = jnp.dot(rows_in, w_gate, preferred_element_type=jnp.float32)
    pre_up = jnp.dot(rows_in, w_up, preferred_element_type=jnp.float32)
    sig_gate = jax.nn.sigmoid(pre_gate)
    silu_gate = pre_gate * sig_gate
    hidden_act = silu_gate * pre_up
    back_grad = lax.dot_general(
        grads_in, w_down, (((1,), (1,)), ((), ())), preferred_element_type=jnp.float32
    )
    row_dots = jnp.sum(hidden_act * back_grad, axis=-1)
    scaled_back = weight_in[:, None] * back_grad
    scaled_act = (weight_in[:, None] * hidden_act).astype(jnp.bfloat16)
    grad_gate = (scaled_back * pre_up * sig_gate * (1.0 + pre_gate * (1.0 - sig_gate))).astype(
        jnp.bfloat16
    )
    grad_up = (scaled_back * silu_gate).astype(jnp.bfloat16)
    sum_gate = lax.dot_general(
        rows_in, grad_gate, (((0,), (0,)), ((), ())), preferred_element_type=jnp.float32
    )
    sum_up = lax.dot_general(
        rows_in, grad_up, (((0,), (0,)), ((), ())), preferred_element_type=jnp.float32
    )
    sum_down = lax.dot_general(
        scaled_act, grads_in, (((0,), (0,)), ((), ())), preferred_element_type=jnp.float32
    )
    partial_input = lax.dot_general(
        grad_gate, w_gate, (((1,), (1,)), ((), ())), preferred_element_type=jnp.float32
    )
    partial_input = partial_input + lax.dot_general(
        grad_up, w_up, (((1,), (1,)), ((), ())), preferred_element_type=jnp.float32
    )
    return (partial_input, row_dots, sum_gate, sum_up, sum_down)


def layer(tokens, out_grad, router_logits, routes, gate_weight, up_weight, down_weight):
    n_dev = lax.axis_size("de")
    n_ha = lax.axis_size("ha")
    core = lax.axis_index("ha")
    tok_rows, model_width = tokens.shape
    route_count = routes.shape[1]
    experts = n_dev * gate_weight.shape[0]
    slot_count = max(2, 5 * tok_rows * route_count // (4 * experts))
    half = -(-slot_count // n_ha)
    slot_count = half * n_ha
    feat = model_width // n_ha
    w_gate = gate_weight[0]
    w_up = up_weight[0]
    w_down = down_weight[0]
    router_probs = jax.nn.softmax(router_logits, axis=-1)
    stride = n_dev // WIN
    dense_cols = []
    for window in range(WIN):
        sent_gate, sent_up, sent_down = (
            spread(w_gate, "de", window * stride),
            spread(w_up, "de", window * stride),
            spread(w_down, "de", window * stride),
        )
        pre_gate = jnp.dot(tokens, sent_gate, preferred_element_type=jnp.float32)
        pre_up = jnp.dot(tokens, sent_up, preferred_element_type=jnp.float32)
        hidden_act = pre_gate * jax.nn.sigmoid(pre_gate) * pre_up
        back_grad = lax.dot_general(
            out_grad, sent_down, (((1,), (1,)), ((), ())), preferred_element_type=jnp.float32
        )
        dense_cols.append(jnp.sum(hidden_act * back_grad, axis=-1))
    dense_dots = lax.psum(jnp.stack(dense_cols, axis=1), "ha")
    route_total = tok_rows * route_count
    total_slots = experts * slot_count
    flat_expert = routes.reshape(-1)
    expert_ids = jnp.arange(experts, dtype=jnp.int32)
    onehot = (flat_expert[:, None] == expert_ids[None, :]).astype(jnp.int32)
    ranking = jnp.sum(jnp.cumsum(onehot, axis=0) * onehot, axis=1) - 1
    slot_of_route = flat_expert * slot_count + ranking
    route_of_slot = (
        jnp.full((total_slots,), route_total, jnp.int32)
        .at[slot_of_route]
        .set(jnp.arange(route_total, dtype=jnp.int32))
    )
    my_routes = lax.dynamic_index_in_dim(
        route_of_slot.reshape(experts, n_ha, half), core, axis=1, keepdims=False
    )
    my_tokens = my_routes // route_count
    route_weight = (
        jnp.take_along_axis(router_probs, routes, axis=1).astype(jnp.bfloat16).reshape(-1)
    )
    padded_tokens = jnp.concatenate([tokens, jnp.zeros((1, model_width), tokens.dtype)])
    padded_grads = jnp.concatenate([out_grad, jnp.zeros((1, model_width), out_grad.dtype)])
    padded_weight = jnp.concatenate([route_weight, jnp.zeros((1,), route_weight.dtype)])
    send_weight = jnp.broadcast_to(
        padded_weight[my_routes][:, :, None], my_routes.shape + (DOT_COLS,)
    )
    send_xg = jnp.concatenate(
        [padded_tokens[my_tokens], padded_grads[my_tokens], send_weight], axis=2
    )
    recv_xg = lax.all_to_all(send_xg, "de", split_axis=0, concat_axis=0, tiled=True)
    all_xg = share_halves(recv_xg, core, n_ha).reshape(-1, 2 * model_width + DOT_COLS)
    rows_in = all_xg[:, :model_width]
    grads_in = all_xg[:, model_width : 2 * model_width]
    weight_in = all_xg[:, 2 * model_width].astype(jnp.float32)
    input_slot, dot_slot, sum_gate, sum_up, sum_down = owner_pass(
        rows_in, grads_in, weight_in, w_gate, w_up, w_down
    )
    dot_slot = lax.psum(dot_slot, "ha")
    input_half = lax.psum_scatter(
        input_slot.reshape(n_ha, n_dev, half, model_width).astype(jnp.bfloat16),
        "ha",
        scatter_dimension=3,
        tiled=True,
    )
    dot_back = jnp.broadcast_to(
        dot_slot.astype(jnp.bfloat16).reshape(n_ha, n_dev, half, 1), (n_ha, n_dev, half, DOT_COLS)
    )
    ret = jnp.concatenate([input_half, dot_back], axis=3)
    ret = jnp.transpose(ret, (1, 0, 2, 3)).reshape(n_dev, slot_count, feat + DOT_COLS)
    back = lax.all_to_all(ret, "de", split_axis=0, concat_axis=0, tiled=True)
    back = back.reshape(total_slots, feat + DOT_COLS)[slot_of_route]
    route_input = back[:, :feat].astype(jnp.float32)
    input_part = jnp.sum(route_input.reshape(tok_rows, route_count, feat), axis=1).astype(
        jnp.bfloat16
    )
    input_grad = lax.all_gather(input_part, "ha", axis=1, tiled=True)
    route_dots = back[:, feat].astype(jnp.float32).reshape(tok_rows, route_count)
    dot_table = jnp.sum(
        jnp.where(routes[:, :, None] == expert_ids[None, None, :], route_dots[:, :, None], 0.0),
        axis=1,
    )
    for window in range(WIN):
        dot_table = jnp.where(
            expert_ids[None, :] == window * stride, dense_dots[:, window : window + 1], dot_table
        )
    logit_grad = router_probs * (
        dot_table - jnp.sum(router_probs * dot_table, axis=-1, keepdims=True)
    )
    return (
        input_grad,
        logit_grad,
        sum_gate.astype(jnp.bfloat16)[None],
        sum_up.astype(jnp.bfloat16)[None],
        sum_down.astype(jnp.bfloat16)[None],
    )


def solution(mesh):
    return jax.shard_map(
        layer,
        mesh=mesh,
        in_specs=(
            P("de", None),
            P("de", None),
            P("de", None),
            P("de", None),
            P("de", None, "ha"),
            P("de", None, "ha"),
            P("de", "ha", None),
        ),
        out_specs=(
            P("de", None),
            P("de", None),
            P("de", None, "ha"),
            P("de", None, "ha"),
            P("de", "ha", None),
        ),
        check_vma=False,
    )
```

```python
import jax
import jax.numpy as jnp
from jax import lax
from jax.sharding import PartitionSpec as P


WIN = 2
DOT_COLS = 128


def spread(value, axis, source):
    kept = jnp.where(lax.axis_index(axis) == source, value, 0).astype(value.dtype)
    return lax.psum(kept, axis)


def share_halves(mine, core, n_ha):
    other = lax.ppermute(mine, "ha", [(i, (i + 1) % n_ha) for i in range(n_ha)])
    first = jnp.where(core == 0, mine, other)
    second = jnp.where(core == 0, other, mine)
    return jnp.stack([first, second])


def owner_pass(rows_in, grads_in, weight_in, w_gate, w_up, w_down):
    pre_gate = jnp.dot(rows_in, w_gate, preferred_element_type=jnp.float32)
    pre_up = jnp.dot(rows_in, w_up, preferred_element_type=jnp.float32)
    sig_gate = jax.nn.sigmoid(pre_gate)
    silu_gate = pre_gate * sig_gate
    hidden_act = silu_gate * pre_up
    back_grad = lax.dot_general(
        grads_in, w_down, (((1,), (1,)), ((), ())), preferred_element_type=jnp.float32
    )
    row_dots = jnp.sum(hidden_act * back_grad, axis=-1)
    scaled_back = weight_in[:, None] * back_grad
    scaled_act = (weight_in[:, None] * hidden_act).astype(jnp.bfloat16)
    grad_gate = (scaled_back * pre_up * sig_gate * (1.0 + pre_gate * (1.0 - sig_gate))).astype(
        jnp.bfloat16
    )
    grad_up = (scaled_back * silu_gate).astype(jnp.bfloat16)
    sum_gate = lax.dot_general(
        rows_in, grad_gate, (((0,), (0,)), ((), ())), preferred_element_type=jnp.float32
    )
    sum_up = lax.dot_general(
        rows_in, grad_up, (((0,), (0,)), ((), ())), preferred_element_type=jnp.float32
    )
    sum_down = lax.dot_general(
        scaled_act, grads_in, (((0,), (0,)), ((), ())), preferred_element_type=jnp.float32
    )
    partial_input = lax.dot_general(
        grad_gate, w_gate, (((1,), (1,)), ((), ())), preferred_element_type=jnp.float32
    )
    partial_input = partial_input + lax.dot_general(
        grad_up, w_up, (((1,), (1,)), ((), ())), preferred_element_type=jnp.float32
    )
    return (partial_input, row_dots, sum_gate, sum_up, sum_down)


def layer(tokens, out_grad, router_logits, routes, gate_weight, up_weight, down_weight):
    n_dev = lax.axis_size("de")
    n_ha = lax.axis_size("ha")
    core = lax.axis_index("ha")
    tok_rows, model_width = tokens.shape
    route_count = routes.shape[1]
    experts = n_dev * gate_weight.shape[0]
    slot_count = max(2, 5 * tok_rows * route_count // (4 * experts))
    half = -(-slot_count // n_ha)
    slot_count = half * n_ha
    feat = model_width // n_ha
    w_gate = gate_weight[0]
    w_up = up_weight[0]
    w_down = down_weight[0]
    router_probs = jax.nn.softmax(router_logits, axis=-1)
    stride = n_dev // WIN
    dense_cols = []
    for window in range(WIN):
        sent_gate, sent_up, sent_down = (
            spread(w_gate, "de", window * stride),
            spread(w_up, "de", window * stride),
            spread(w_down, "de", window * stride),
        )
        pre_gate = jnp.dot(tokens, sent_gate, preferred_element_type=jnp.float32)
        pre_up = jnp.dot(tokens, sent_up, preferred_element_type=jnp.float32)
        hidden_act = pre_gate * jax.nn.sigmoid(pre_gate) * pre_up
        back_grad = lax.dot_general(
            out_grad, sent_down, (((1,), (1,)), ((), ())), preferred_element_type=jnp.float32
        )
        dense_cols.append(jnp.sum(hidden_act * back_grad, axis=-1))
    dense_dots = lax.psum(jnp.stack(dense_cols, axis=1), "ha")
    route_total = tok_rows * route_count
    total_slots = experts * slot_count
    flat_expert = routes.reshape(-1)
    expert_ids = jnp.arange(experts, dtype=jnp.int32)
    onehot = (flat_expert[:, None] == expert_ids[None, :]).astype(jnp.int32)
    ranking = jnp.sum(jnp.cumsum(onehot, axis=0) * onehot, axis=1) - 1
    slot_of_route = flat_expert * slot_count + ranking
    route_of_slot = (
        jnp.full((total_slots,), route_total, jnp.int32)
        .at[slot_of_route]
        .set(jnp.arange(route_total, dtype=jnp.int32))
    )
    my_routes = lax.dynamic_index_in_dim(
        route_of_slot.reshape(experts, n_ha, half), core, axis=1, keepdims=False
    )
    my_tokens = my_routes // route_count
    route_weight = (
        jnp.take_along_axis(router_probs, routes, axis=1).astype(jnp.bfloat16).reshape(-1)
    )
    padded_tokens = jnp.concatenate([tokens, jnp.zeros((1, model_width), tokens.dtype)])
    padded_grads = jnp.concatenate([out_grad, jnp.zeros((1, model_width), out_grad.dtype)])
    padded_weight = jnp.concatenate([route_weight, jnp.zeros((1,), route_weight.dtype)])
    send_weight = jnp.broadcast_to(
        padded_weight[my_routes][:, :, None], my_routes.shape + (DOT_COLS,)
    )
    send_xg = jnp.concatenate(
        [padded_tokens[my_tokens], padded_grads[my_tokens], send_weight], axis=2
    )
    recv_xg = lax.all_to_all(send_xg, "de", split_axis=0, concat_axis=0, tiled=True)
    all_xg = share_halves(recv_xg, core, n_ha).reshape(-1, 2 * model_width + DOT_COLS)
    rows_in = all_xg[:, :model_width]
    grads_in = all_xg[:, model_width : 2 * model_width]
    weight_in = all_xg[:, 2 * model_width].astype(jnp.float32)
    input_slot, dot_slot, sum_gate, sum_up, sum_down = owner_pass(
        rows_in, grads_in, weight_in, w_gate, w_up, w_down
    )
    dot_slot = lax.psum(dot_slot, "ha")
    input_half = lax.psum_scatter(
        input_slot.reshape(n_ha, n_dev, half, model_width).astype(jnp.bfloat16),
        "ha",
        scatter_dimension=3,
        tiled=True,
    )
    dot_back = jnp.broadcast_to(
        dot_slot.astype(jnp.bfloat16).reshape(n_ha, n_dev, half, 1), (n_ha, n_dev, half, DOT_COLS)
    )
    ret = jnp.concatenate([input_half, dot_back], axis=3)
    ret = jnp.transpose(ret, (1, 0, 2, 3)).reshape(n_dev, slot_count, feat + DOT_COLS)
    back = lax.all_to_all(ret, "de", split_axis=0, concat_axis=0, tiled=True)
    back = back.reshape(total_slots, feat + DOT_COLS)[slot_of_route]
    route_input = back[:, :feat].astype(jnp.float32)
    input_part = jnp.sum(route_input.reshape(tok_rows, route_count, feat), axis=1).astype(
        jnp.bfloat16
    )
    input_grad = lax.all_gather(input_part, "ha", axis=1, tiled=True)
    route_dots = back[:, feat].astype(jnp.float32).reshape(tok_rows, route_count)
    dot_table = jnp.sum(
        jnp.where(routes[:, :, None] == expert_ids[None, None, :], route_dots[:, :, None], 0.0),
        axis=1,
    )
    for window in range(WIN):
        dot_table = jnp.where(
            expert_ids[None, :] == window * stride, dense_dots[:, window : window + 1], dot_table
        )
    logit_grad = router_probs * (
        dot_table - jnp.sum(router_probs * dot_table, axis=-1, keepdims=True)
    )
    return (
        input_grad,
        logit_grad,
        sum_gate.astype(jnp.bfloat16)[None],
        sum_up.astype(jnp.bfloat16)[None],
        sum_down.astype(jnp.bfloat16)[None],
    )


def solution(mesh):
    return jax.shard_map(
        layer,
        mesh=mesh,
        in_specs=(
            P("de", None),
            P("de", None),
            P("de", None),
            P("de", None),
            P("de", None, "ha"),
            P("de", None, "ha"),
            P("de", "ha", None),
        ),
        out_specs=(
            P("de", None),
            P("de", None),
            P("de", None, "ha"),
            P("de", None, "ha"),
            P("de", "ha", None),
        ),
        check_vma=False,
    )
```

```python
import jax
import jax.numpy as jnp
from jax import lax
from jax.sharding import PartitionSpec as P


WIN = 2
DOT_COLS = 128


def spread(value, axis, source):
    kept = jnp.where(lax.axis_index(axis) == source, value, 0).astype(value.dtype)
    return lax.psum(kept, axis)


def share_halves(mine, core, n_ha):
    other = lax.ppermute(mine, "ha", [(i, (i + 1) % n_ha) for i in range(n_ha)])
    full = jnp.zeros((n_ha,) + mine.shape, mine.dtype)
    full = lax.dynamic_update_index_in_dim(full, mine, core, 0)
    return lax.dynamic_update_index_in_dim(full, other, 1 - core, 0)


def owner_pass(rows_in, grads_in, weight_in, w_gate, w_up, w_down):
    pre_gate = jnp.dot(rows_in, w_gate, preferred_element_type=jnp.float32)
    pre_up = jnp.dot(rows_in, w_up, preferred_element_type=jnp.float32)
    sig_gate = jax.nn.sigmoid(pre_gate)
    silu_gate = pre_gate * sig_gate
    hidden_act = silu_gate * pre_up
    back_grad = lax.dot_general(
        grads_in, w_down, (((1,), (1,)), ((), ())), preferred_element_type=jnp.float32
    )
    row_dots = jnp.sum(hidden_act * back_grad, axis=-1)
    scaled_back = weight_in[:, None] * back_grad
    scaled_act = (weight_in[:, None] * hidden_act).astype(jnp.bfloat16)
    grad_gate = (scaled_back * pre_up * sig_gate * (1.0 + pre_gate * (1.0 - sig_gate))).astype(
        jnp.bfloat16
    )
    grad_up = (scaled_back * silu_gate).astype(jnp.bfloat16)
    sum_gate = lax.dot_general(
        rows_in, grad_gate, (((0,), (0,)), ((), ())), preferred_element_type=jnp.float32
    )
    sum_up = lax.dot_general(
        rows_in, grad_up, (((0,), (0,)), ((), ())), preferred_element_type=jnp.float32
    )
    sum_down = lax.dot_general(
        scaled_act, grads_in, (((0,), (0,)), ((), ())), preferred_element_type=jnp.float32
    )
    partial_input = lax.dot_general(
        grad_gate, w_gate, (((1,), (1,)), ((), ())), preferred_element_type=jnp.float32
    )
    partial_input = partial_input + lax.dot_general(
        grad_up, w_up, (((1,), (1,)), ((), ())), preferred_element_type=jnp.float32
    )
    return (partial_input, row_dots, sum_gate, sum_up, sum_down)


def layer(tokens, out_grad, router_logits, routes, gate_weight, up_weight, down_weight):
    n_dev = lax.axis_size("de")
    n_ha = lax.axis_size("ha")
    core = lax.axis_index("ha")
    tok_rows, model_width = tokens.shape
    route_count = routes.shape[1]
    experts = n_dev * gate_weight.shape[0]
    slot_count = max(2, 5 * tok_rows * route_count // (4 * experts))
    half = -(-slot_count // n_ha)
    slot_count = half * n_ha
    feat = model_width // n_ha
    w_gate = gate_weight[0]
    w_up = up_weight[0]
    w_down = down_weight[0]
    router_probs = jax.nn.softmax(router_logits, axis=-1)
    stride = n_dev // WIN
    dense_cols = []
    for window in range(WIN):
        sent_gate, sent_up, sent_down = (
            spread(w_gate, "de", window * stride),
            spread(w_up, "de", window * stride),
            spread(w_down, "de", window * stride),
        )
        pre_gate = jnp.dot(tokens, sent_gate, preferred_element_type=jnp.float32)
        pre_up = jnp.dot(tokens, sent_up, preferred_element_type=jnp.float32)
        hidden_act = pre_gate * jax.nn.sigmoid(pre_gate) * pre_up
        back_grad = lax.dot_general(
            out_grad, sent_down, (((1,), (1,)), ((), ())), preferred_element_type=jnp.float32
        )
        dense_cols.append(jnp.sum(hidden_act * back_grad, axis=-1))
    dense_dots = lax.psum(jnp.stack(dense_cols, axis=1), "ha")
    route_total = tok_rows * route_count
    total_slots = experts * slot_count
    flat_expert = routes.reshape(-1)
    expert_ids = jnp.arange(experts, dtype=jnp.int32)
    onehot = (flat_expert[:, None] == expert_ids[None, :]).astype(jnp.int32)
    ranking = jnp.sum(jnp.cumsum(onehot, axis=0) * onehot, axis=1) - 1
    slot_of_route = flat_expert * slot_count + ranking
    route_of_slot = (
        jnp.full((total_slots,), route_total, jnp.int32)
        .at[slot_of_route]
        .set(jnp.arange(route_total, dtype=jnp.int32))
    )
    my_routes = lax.dynamic_index_in_dim(
        route_of_slot.reshape(experts, n_ha, half), core, axis=1, keepdims=False
    )
    my_tokens = my_routes // route_count
    route_weight = (
        jnp.take_along_axis(router_probs, routes, axis=1).astype(jnp.bfloat16).reshape(-1)
    )
    padded_tokens = jnp.concatenate([tokens, jnp.zeros((1, model_width), tokens.dtype)])
    padded_grads = jnp.concatenate([out_grad, jnp.zeros((1, model_width), out_grad.dtype)])
    padded_weight = jnp.concatenate([route_weight, jnp.zeros((1,), route_weight.dtype)])
    send_weight = jnp.broadcast_to(
        padded_weight[my_routes][:, :, None], my_routes.shape + (DOT_COLS,)
    )
    send_xg = jnp.concatenate(
        [padded_tokens[my_tokens], padded_grads[my_tokens], send_weight], axis=2
    )
    recv_xg = lax.all_to_all(send_xg, "de", split_axis=0, concat_axis=0, tiled=True)
    all_xg = share_halves(recv_xg, core, n_ha).reshape(-1, 2 * model_width + DOT_COLS)
    rows_in = all_xg[:, :model_width]
    grads_in = all_xg[:, model_width : 2 * model_width]
    weight_in = all_xg[:, 2 * model_width].astype(jnp.float32)
    input_slot, dot_slot, sum_gate, sum_up, sum_down = owner_pass(
        rows_in, grads_in, weight_in, w_gate, w_up, w_down
    )
    dot_slot = lax.psum(dot_slot, "ha")
    input_half = lax.psum_scatter(
        input_slot.reshape(n_ha, n_dev, half, model_width).astype(jnp.bfloat16),
        "ha",
        scatter_dimension=3,
        tiled=True,
    )
    dot_back = jnp.transpose(
        dot_slot.astype(jnp.bfloat16).reshape(n_ha, n_dev, half), (1, 0, 2)
    ).reshape(n_dev, slot_count)
    ret = jnp.transpose(input_half, (1, 0, 2, 3)).reshape(n_dev, slot_count, feat)
    back = lax.all_to_all(ret, "de", split_axis=0, concat_axis=0, tiled=True)
    back_dots = lax.all_to_all(dot_back, "de", split_axis=0, concat_axis=0, tiled=True)
    back = back.reshape(total_slots, feat)[slot_of_route]
    route_input = back[:, :feat].astype(jnp.float32)
    input_part = jnp.sum(route_input.reshape(tok_rows, route_count, feat), axis=1).astype(
        jnp.bfloat16
    )
    input_grad = lax.all_gather(input_part, "ha", axis=1, tiled=True)
    route_dots = (
        back_dots.reshape(total_slots)[slot_of_route]
        .astype(jnp.float32)
        .reshape(tok_rows, route_count)
    )
    dot_table = jnp.sum(
        jnp.where(routes[:, :, None] == expert_ids[None, None, :], route_dots[:, :, None], 0.0),
        axis=1,
    )
    for window in range(WIN):
        dot_table = jnp.where(
            expert_ids[None, :] == window * stride, dense_dots[:, window : window + 1], dot_table
        )
    logit_grad = router_probs * (
        dot_table - jnp.sum(router_probs * dot_table, axis=-1, keepdims=True)
    )
    return (
        input_grad,
        logit_grad,
        sum_gate.astype(jnp.bfloat16)[None],
        sum_up.astype(jnp.bfloat16)[None],
        sum_down.astype(jnp.bfloat16)[None],
    )


def solution(mesh):
    return jax.shard_map(
        layer,
        mesh=mesh,
        in_specs=(
            P("de", None),
            P("de", None),
            P("de", None),
            P("de", None),
            P("de", None, "ha"),
            P("de", None, "ha"),
            P("de", "ha", None),
        ),
        out_specs=(
            P("de", None),
            P("de", None),
            P("de", None, "ha"),
            P("de", None, "ha"),
            P("de", "ha", None),
        ),
        check_vma=False,
    )
```
